32 devices in a mesh: groups: 2 (over y), replica: 4 (over z), tensor: 4 (over x, core).
Axes of the slice: x: 2, y: 2, z: 4, core: 2. Of those that a mesh axis runs over, the one named last changes fastest.
Arguments:
- queries: bfloat16 [144, 8192], P(('groups', 'replica'), 'tensor'), parts along dimension 0, may hold values from -64 to 64
- past_cache: bfloat16 [2, 144, 128, 1024], P(None, ('groups', 'replica'), None, 'tensor'), parts along dimension 1, may hold values from -6 to 6
- lengths: int32 [144], P(('groups', 'replica')), parts along dimension 0, may hold values from 2 to 128, as said below
- live_counts: int32 [8], P(('groups', 'replica')), parts along dimension 0, may hold values from 1 to 16, as said below
- adapter_index: int32 [144], P(('groups', 'replica')), parts along dimension 0, may hold values from 0 to 15, as said below
- adapter_down: bfloat16 [16, 16, 8192], P('replica', None, 'tensor'), may hold values from -0.0625 to 0.0625
- adapter_up: bfloat16 [16, 16, 8192], P('replica', None, 'tensor'), may hold values from -6 to 6
Outputs:
- attention: bfloat16 [144, 8192], P(('groups', 'replica'), 'tensor'), parts along dimension 0
- adapted: bfloat16 [144, 8192], P(('groups', 'replica'), 'tensor'), parts along dimension 0
The draws below stay inside these ranges and needn't reach their ends.
There are 2 independent parts, one for each index of `groups`. The reference program is written for one: setup_inputs(seed, part) draws one part's arguments, and reference() takes and returns one part's arrays. A program takes and returns all parts, laid end to end along the dimension named above; an argument that names none is the same for every part. Nothing has to cross between parts.
Inputs may be any that keep to these rules, and one draw needn't show every extreme that they name: `adapter_index`: over the first 16 slots of all replicas, exactly 4 distinct adapters appear, homed on 4 distinct replicas. Each of the last 2 slots of a replica names an adapter outside that set; the homes (adapter a lives on replica a // 4) of one replica's last 2 slots are distinct, and some replica is the home of one such slot of every replica. `lengths`: some request has exactly 128. `live_counts`: some replica has exactly 16.
All inputs are finite; a program needn't handle non-finite values.
Results may differ from the reference program's by a relative error of at most 0.008.
Values may be sent and summed in bfloat16 or wider, within the bound.
A program may use at most 64 MiB of HBM per device.

```python
import math
import jax
import jax.numpy as jnp
from jax import lax

D = 8192
HEADS = 64
KV_HEADS = 8
HEAD_DIM = 128
RANK = 16
ADP_DEV = 4
STAY = 16
CONTEXT = 128
HOT = 4
MIG = 2
B_DEV = 18
ADAPTERS = 16
REQUESTS = 72
N_REPLICA = 4


def routing(key):
    base = jax.random.fold_in(key, 11)
    streams = jax.random.split(base, 8)
    replicas = N_REPLICA
    lower_half = replicas // 2
    hot_homes = jax.random.permutation(streams[0], replicas)[:HOT].astype(jnp.int32)
    hot_local = jax.random.randint(streams[1], (HOT,), 0, ADP_DEV, dtype=jnp.int32)
    hot_ids = hot_homes * ADP_DEV + hot_local
    marks = jnp.full((replicas,), -1, jnp.int32).at[hot_homes].set(hot_local)
    picks = jax.random.randint(streams[2], (replicas, STAY), 0, HOT, dtype=jnp.int32)
    lower_picks = jax.random.randint(jax.random.fold_in(base, 101), (replicas, STAY), 1, HOT, dtype=jnp.int32)
    row_ids = jnp.arange(replicas, dtype=jnp.int32)
    picks = jnp.where((row_ids < lower_half)[:, None], lower_picks, picks)
    stay_ids = hot_ids[picks]
    first_row = jax.random.randint(streams[3], (), lower_half, replicas, dtype=jnp.int32)
    stay_ids = stay_ids.at[first_row, :HOT].set(hot_ids)
    full_home = jax.random.randint(streams[4], (), 0, replicas, dtype=jnp.int32)

    def choose(row_key):
        order = jax.random.permutation(row_key, replicas).astype(jnp.int32)[:MIG]
        present = jnp.any(order == full_home)
        return jnp.where(present, order, order.at[MIG - 1].set(full_home))
    targets = jax.vmap(choose)(jax.random.split(streams[5], replicas))
    spare = jax.random.randint(streams[6], (replicas, MIG), 0, ADP_DEV - 1, dtype=jnp.int32)
    loose = jax.random.randint(streams[7], (replicas, MIG), 0, ADP_DEV, dtype=jnp.int32)
    marked = marks[targets]
    local = jnp.where(marked < 0, loose, spare + (spare >= marked).astype(jnp.int32))
    moved_ids = targets * ADP_DEV + local
    return jnp.concatenate([stay_ids, moved_ids], axis=1).reshape(REQUESTS)


def draw_adapter_index(key, part):
    return routing(key)


def draw_lengths(key, part):
    base = jax.random.fold_in(key, 23)
    values = jax.random.randint(base, (REQUESTS,), 2, CONTEXT + 1, dtype=jnp.int32)
    position = jax.random.randint(jax.random.fold_in(base, 1), (), 0, REQUESTS, dtype=jnp.int32)
    return values.at[position].set(CONTEXT)


def draw_live_counts(key, part):
    base = jax.random.fold_in(key, 29)
    values = jax.random.randint(base, (N_REPLICA,), 1, STAY + 1, dtype=jnp.int32)
    position = jax.random.randint(jax.random.fold_in(base, 1), (), 0, N_REPLICA, dtype=jnp.int32)
    return values.at[position].set(STAY)


def paired_draws(key):
    base = jax.random.fold_in(key, 37)
    streams = jax.random.split(base, 2)
    width = KV_HEADS * HEAD_DIM
    queries = jax.random.truncated_normal(streams[0], -6.0, 6.0, (REQUESTS, HEADS * HEAD_DIM), jnp.float32)
    cache = jax.random.truncated_normal(streams[1], -6.0, 6.0, (2, REQUESTS, CONTEXT, width), jnp.float32)
    return (queries, cache)


def draw_queries(key, part):
    return paired_draws(key)[0].astype(jnp.bfloat16)


def draw_past_cache(key, part):
    return paired_draws(key)[1].astype(jnp.bfloat16)


def block_scale(rng, dims, cuts, low, top_value):
    gain, own = 1.0, jax.random.fold_in(rng, 6)
    for dim, parts in cuts:
        steps = jnp.exp(jax.random.uniform(jax.random.fold_in(own, dim), (parts,), jnp.float32, low / len(cuts), top_value / len(cuts)))
        gain = gain * jnp.repeat(steps, dims[dim] // parts).reshape([-1 if axis == dim else 1 for axis in range(len(dims))])
    return gain


def noise(key, extent, spread, limit, shards=(), kind=jnp.bfloat16):
    entries = spread * jax.random.normal(key, extent, jnp.float32)
    if shards:
        entries = entries * block_scale(key, extent, shards, -0.22, 0.18)
    return jnp.clip(entries, -limit, limit).astype(kind)


def setup_inputs(seed: int = 0, part: int = 0) -> dict:
    key_list = jax.random.split(jax.random.key(seed), 8)
    part_splits = jax.random.split(jax.random.fold_in(key_list[7], part), 8)
    queries = draw_queries(jax.random.fold_in(jax.random.fold_in(key_list[7], part), 71), part)
    past_cache = draw_past_cache(jax.random.fold_in(jax.random.fold_in(key_list[7], part), 71), part)
    lengths = draw_lengths(jax.random.fold_in(jax.random.fold_in(key_list[7], part), 71), part)
    live_counts = draw_live_counts(jax.random.fold_in(jax.random.fold_in(key_list[7], part), 71), part)
    adapter_index = draw_adapter_index(jax.random.fold_in(jax.random.fold_in(key_list[7], part), 71), part)
    adapter_down = noise(key_list[5], (ADAPTERS, RANK, HEADS * HEAD_DIM), (HEADS * HEAD_DIM) ** -0.5, 0.0625, ((0, 4), (2, 4)))
    adapter_up = noise(key_list[6], (ADAPTERS, RANK, D), 1.0, 6.0, ((0, 4), (2, 4)))
    return dict(queries=queries, past_cache=past_cache, lengths=lengths, live_counts=live_counts, adapter_index=adapter_index, adapter_down=adapter_down, adapter_up=adapter_up)


SCALING = 2.0

def attend_block(queries, keys, values, visible):
    count = queries.shape[0]
    key_width = keys.shape[-1]
    key_heads = key_width // HEAD_DIM
    group_size = queries.shape[1] // key_width
    context = keys.shape[1]
    query_rows = queries.astype(jnp.float32).reshape(count, key_heads, group_size, HEAD_DIM)
    key_rows = keys.astype(jnp.float32).reshape(count, context, key_heads, HEAD_DIM)
    value_rows = values.astype(jnp.float32).reshape(count, context, key_heads, HEAD_DIM)
    scores = jnp.einsum('nhgd,nlhd->nhgl', query_rows, key_rows) / math.sqrt(HEAD_DIM)
    scores = jnp.where(visible[:, None, None, :], scores, -jnp.inf)
    peak = lax.optimization_barrier(jnp.max(scores, axis=-1, keepdims=True))
    raised = jnp.exp(scores - peak)
    weights = (raised / lax.optimization_barrier(jnp.sum(raised, axis=-1, keepdims=True))).astype(jnp.bfloat16)
    mixed = jnp.einsum('nhgl,nlhd->nhgd', weights.astype(jnp.float32), value_rows)
    return mixed.reshape(count, key_heads * group_size * HEAD_DIM)

def reference(queries, past_cache, lengths, live_counts, adapter_index, adapter_down, adapter_up):
    requests = queries.shape[0]
    blocks = requests // B_DEV
    width = past_cache.shape[-1]
    slot_index = jnp.arange(requests, dtype=jnp.int32) % B_DEV
    owner = jnp.arange(requests, dtype=jnp.int32) // B_DEV
    alive = (slot_index >= STAY) | (slot_index < live_counts[owner])
    position = jnp.arange(CONTEXT, dtype=jnp.int32)
    zero = jnp.zeros((), jnp.int32)

    def one_block(block):
        start = (block * B_DEV).astype(jnp.int32)
        block_queries = lax.dynamic_slice_in_dim(queries, start, B_DEV, 0)
        block_cache = lax.dynamic_slice(past_cache, (zero, start, zero, zero), (2, B_DEV, CONTEXT, width))
        block_lengths = lax.dynamic_slice_in_dim(lengths, start, B_DEV, 0)
        block_alive = lax.dynamic_slice_in_dim(alive, start, B_DEV, 0)
        visible = position[None, :] < block_lengths[:, None]
        mixed = attend_block(block_queries, block_cache[0], block_cache[1], visible)
        attention = jnp.where(block_alive[:, None], mixed, 0.0).astype(jnp.bfloat16)
        chosen = lax.dynamic_slice_in_dim(adapter_index, start, B_DEV, 0)
        down_rows = adapter_down[chosen].astype(jnp.float32)
        up_rows = adapter_up[chosen].astype(jnp.float32)
        rank_rows = jnp.einsum('nc,nrc->nr', attention.astype(jnp.float32), down_rows)
        adapted = (SCALING * jnp.einsum('nr,nrc->nc', rank_rows, up_rows)).astype(jnp.bfloat16)
        return (attention, adapted)
    attention, adapted = lax.map(one_block, jnp.arange(blocks, dtype=jnp.int32))
    return (attention.reshape(requests, -1), adapted.reshape(requests, -1))
```

```python
import functools
import math

import jax
import jax.numpy as jnp
from jax import lax
from jax.experimental import pallas as pl
from jax.experimental.pallas import tpu as pltpu
from jax.sharding import PartitionSpec as P

HEAD_DIM = 128
STAY = 16
SCALING = 2.0
GROUP = 4
MESH = pl.DeviceIdType.MESH
F32 = jnp.float32
BF16 = jnp.bfloat16


def dot_nt(a, b):
    return lax.dot_general(a, b, (((1,), (1,)), ((), ())), preferred_element_type=F32)


def dot_nn(a, b):
    return lax.dot_general(a, b, (((1,), (0,)), ((), ())), preferred_element_type=F32)


def widen(ranks, up):
    high = ranks.astype(BF16)
    low = (ranks - high.astype(F32)).astype(BF16)
    return SCALING * (dot_nn(high, up) + dot_nn(low, up))


def kernel(
    replicas, tensors,
    lengths, live, index, queries, cache, down, up,
    attention, adapted,
    q_in, kv, down_v, up_v, q_rows, o_rows,
    idx_buf, row_out, row_in, row_send, row_back, hot_down, hot_up, rank_m, rank_s,
    local_sem, group_sem,
    idx_s, idx_r, row_s, row_r, back_s, back_r, hd_s, hd_r, hu_s, hu_r, tm_s, tm_r, ts_s, ts_r,
):
    me = lax.axis_index("replica")
    mine = lax.axis_index("tensor")
    slots, cols = queries.shape
    moving = slots - STAY
    context = cache.shape[2]
    key_heads = cache.shape[3] // HEAD_DIM
    heads = cols // HEAD_DIM
    size = heads // key_heads
    count, rank = down.shape[0], down.shape[1]
    groups = STAY // GROUP

    def peer(offset):
        return {"replica": lax.rem(me + offset, replicas)}

    def side(offset):
        return {"tensor": lax.rem(mine + offset, tensors)}

    barrier = pltpu.get_barrier_semaphore()
    for d in range(1, replicas):
        pl.semaphore_signal(barrier, inc=1, device_id=peer(d), device_id_type=MESH)
    for d in range(1, tensors):
        pl.semaphore_signal(barrier, inc=1, device_id=side(d), device_id_type=MESH)

    load_q = pltpu.make_async_copy(queries, q_in, local_sem.at[0])
    load_m = pltpu.make_async_copy(
        cache.at[:, pl.ds(STAY, moving)], kv.at[:, pl.ds(STAY, moving)], local_sem.at[1]
    )
    load_d = pltpu.make_async_copy(down, down_v, local_sem.at[2])
    load_u = pltpu.make_async_copy(up, up_v, local_sem.at[3])
    loads = [
        pltpu.make_async_copy(
            cache.at[:, pl.ds(g * GROUP, GROUP)], kv.at[:, pl.ds(g * GROUP, GROUP)], group_sem.at[g]
        )
        for g in range(groups)
    ]
    load_q.start()
    load_m.start()
    for copy in loads[:2]:
        copy.start()
    load_d.start()
    load_u.start()
    for copy in loads[2:]:
        copy.start()

    def to_peers(source, target, send, recv):
        return [
            pltpu.make_async_remote_copy(
                src_ref=source(d), dst_ref=target.at[d], send_sem=send.at[d - 1],
                recv_sem=recv.at[d - 1], device_id=peer(d), device_id_type=MESH,
            )
            for d in range(1, replicas)
        ]

    def to_sides(buffer, send, recv):
        return [
            pltpu.make_async_remote_copy(
                src_ref=buffer.at[0], dst_ref=buffer.at[d], send_sem=send.at[d - 1],
                recv_sem=recv.at[d - 1], device_id=side(d), device_id_type=MESH,
            )
            for d in range(1, tensors)
        ]

    send_idx = to_peers(lambda d: idx_buf.at[0], idx_buf, idx_s, idx_r)
    send_rows = to_peers(lambda d: row_out.at[d], row_in, row_s, row_r)
    send_hd = to_peers(lambda d: hot_down.at[0], hot_down, hd_s, hd_r)
    send_hu = to_peers(lambda d: hot_up.at[0], hot_up, hu_s, hu_r)
    send_back = [
        pltpu.make_async_remote_copy(
            src_ref=row_send.at[d], dst_ref=row_back.at[d], send_sem=back_s.at[d - 1],
            recv_sem=back_r.at[d - 1], device_id=peer(replicas - d), device_id_type=MESH,
        )
        for d in range(1, replicas)
    ]
    send_tm = to_sides(rank_m, tm_s, tm_r)
    send_ts = to_sides(rank_s, ts_s, ts_r)

    lane = lax.broadcasted_iota(jnp.int32, (1, 128), 1)
    line = jnp.full((1, 128), -1, jnp.int32)
    for i in range(slots):
        line = jnp.where(lane == i, index[i], line)
    idx_buf[0] = line
    stay_row = lax.broadcasted_iota(jnp.int32, (STAY, 1), 0)
    stay_rel = jnp.zeros((STAY, 1), jnp.int32)
    for i in range(STAY):
        stay_rel = jnp.where(stay_row == i, lax.rem(me - index[i] // count + replicas, replicas), stay_rel)
    move_rel = [lax.rem(index[STAY + j] // count - me + replicas, replicas) for j in range(moving)]

    load_q.wait()
    for h in range(heads):
        q_rows[pl.ds(h, slots, stride=heads), :] = q_in[:, h * HEAD_DIM:(h + 1) * HEAD_DIM].astype(F32)

    head_row = lax.broadcasted_iota(jnp.int32, (heads, 1), 0) // size
    position = lax.broadcasted_iota(jnp.int32, (1, context), 1)

    def attend(requests):
        for n in requests:
            q = q_rows[n * heads:(n + 1) * heads, :]
            wide = jnp.concatenate(
                [jnp.where(head_row == g, q, 0.0) for g in range(key_heads)], axis=1
            ).astype(BF16)
            scores = dot_nt(wide, kv[0, n]) / math.sqrt(HEAD_DIM)
            scores = jnp.where(position < lengths[n], scores, -jnp.inf)
            peak = jnp.max(scores, axis=-1, keepdims=True)
            raised = jnp.exp(scores - peak)
            weights = (raised / jnp.sum(raised, axis=-1, keepdims=True)).astype(BF16)
            mixed = dot_nn(weights, kv[1, n])
            out = jnp.zeros((heads, HEAD_DIM), F32)
            for g in range(key_heads):
                out = jnp.where(head_row == g, mixed[:, g * HEAD_DIM:(g + 1) * HEAD_DIM], out)
            o_rows[n * heads:(n + 1) * heads, :] = out

    def gather_rows(first, number):
        return jnp.concatenate(
            [o_rows[pl.ds(first * heads + h, number, stride=heads), :] for h in range(heads)], axis=1
        )

    load_m.wait()
    attend(range(STAY, slots))
    moved = gather_rows(STAY, moving).astype(BF16)
    attention[STAY:slots, :] = moved
    moved = moved.astype(F32)
    replica_row = lax.broadcasted_iota(jnp.int32, (replicas, 1), 0)
    picked = jnp.zeros((replicas, cols), F32)
    for j in range(moving):
        picked = jnp.where(replica_row == move_rel[j], moved[j:j + 1, :], picked)
    row_in[0] = picked[0:1, :]
    for d in range(1, replicas):
        row_out[d] = picked[d:d + 1, :]

    pl.semaphore_wait(barrier, replicas - 1 + tensors - 1)
    for copy in send_idx:
        copy.start()
    for copy in send_rows:
        copy.start()

    for g in range(groups // 2):
        loads[g].wait()
        attend(range(g * GROUP, (g + 1) * GROUP))

    load_d.wait()
    load_u.wait()
    for copy in send_idx:
        copy.wait_recv()
    table = jnp.concatenate([idx_buf[d] for d in range(replicas)], axis=0)
    here = (table >= 0) & (table // count == me)
    local = jnp.where(here, table - me * count, -1)
    lanes = lax.broadcasted_iota(jnp.int32, table.shape, 1)
    hot = jnp.maximum(jnp.max(jnp.where(lanes < STAY, local, -1)), 0)
    hot_down[0] = down_v[hot]
    hot_up[0] = up_v[hot]
    for copy in send_hd:
        copy.start()
    for copy in send_hu:
        copy.start()

    asked = jnp.max(jnp.where(lanes >= STAY, local, -1), axis=1, keepdims=True)
    for copy in send_rows:
        copy.wait_recv()
    rows = jnp.concatenate([row_in[d] for d in range(replicas)], axis=0).astype(BF16)
    partial = dot_nt(rows, down_v[...].reshape(count * rank, cols))
    owner = lax.broadcasted_iota(jnp.int32, partial.shape, 1) // rank
    rank_m[0] = jnp.where(owner == asked, partial, 0.0)
    for copy in send_tm:
        copy.start()

    for g in range(groups // 2, groups):
        loads[g].wait()
        attend(range(g * GROUP, (g + 1) * GROUP))

    for copy in send_tm:
        copy.wait_recv()
    total = rank_m[0]
    for d in range(1, tensors):
        total = total + rank_m[d]
    made = widen(total, up_v[...].reshape(count * rank, cols)).astype(BF16).astype(F32)
    row_back[0] = made[0:1, :]
    for d in range(1, replicas):
        row_send[d] = made[d:d + 1, :]
    for copy in send_back:
        copy.start()

    stay = jnp.where(stay_row < live[0], gather_rows(0, STAY), 0.0).astype(BF16)
    attention[0:STAY, :] = stay

    for copy in send_hd:
        copy.wait_recv()
    partial = dot_nt(stay, hot_down[...].reshape(replicas * rank, cols))
    owner = lax.broadcasted_iota(jnp.int32, partial.shape, 1) // rank
    rank_s[0] = jnp.where(owner == stay_rel, partial, 0.0)
    for copy in send_ts:
        copy.start()

    for copy in send_back:
        copy.wait_recv()
    back = jnp.concatenate([row_back[d] for d in range(replicas)], axis=0)
    adapted[STAY:slots, :] = jnp.concatenate(
        [
            jnp.sum(jnp.where(replica_row == move_rel[j], back, 0.0), axis=0, keepdims=True)
            for j in range(moving)
        ],
        axis=0,
    ).astype(BF16)

    for copy in send_ts:
        copy.wait_recv()
    total = rank_s[0]
    for d in range(1, tensors):
        total = total + rank_s[d]
    for copy in send_hu:
        copy.wait_recv()
    adapted[0:STAY, :] = widen(total, hot_up[...].reshape(replicas * rank, cols)).astype(BF16)

    for copy in send_idx + send_rows + send_hd + send_hu + send_back + send_tm + send_ts:
        copy.wait_send()


def on_device(replicas, tensors, queries, past_cache, lengths, live_counts, adapter_index, adapter_down, adapter_up):
    slots, cols = queries.shape
    count, rank = adapter_down.shape[0], adapter_down.shape[1]
    heads = cols // HEAD_DIM
    out = jax.ShapeDtypeStruct((slots, cols), BF16)
    smem = pl.BlockSpec(memory_space=pltpu.SMEM)
    anywhere = pl.BlockSpec(memory_space=pl.ANY)
    vmem = pl.BlockSpec(memory_space=pltpu.VMEM)
    dma = pltpu.SemaphoreType.DMA
    rep = dma((max(replicas - 1, 1),))
    ten = dma((max(tensors - 1, 1),))
    scratch = [
        pltpu.VMEM((slots, cols), BF16),
        pltpu.VMEM(past_cache.shape, BF16),
        pltpu.VMEM(adapter_down.shape, BF16),
        pltpu.VMEM(adapter_up.shape, BF16),
        pltpu.VMEM((slots * heads, HEAD_DIM), F32),
        pltpu.VMEM((slots * heads, HEAD_DIM), F32),
        pltpu.VMEM((replicas, 1, 128), jnp.int32),
        pltpu.VMEM((replicas, 1, cols), F32),
        pltpu.VMEM((replicas, 1, cols), F32),
        pltpu.VMEM((replicas, 1, cols), F32),
        pltpu.VMEM((replicas, 1, cols), F32),
        pltpu.VMEM((replicas, rank, cols), BF16),
        pltpu.VMEM((replicas, rank, cols), BF16),
        pltpu.VMEM((tensors, replicas, count * rank), F32),
        pltpu.VMEM((tensors, STAY, replicas * rank), F32),
        dma((4,)),
        dma((STAY // GROUP,)),
        rep, rep, rep, rep, rep, rep, rep, rep, rep, rep, ten, ten, ten, ten,
    ]
    return pl.pallas_call(
        functools.partial(kernel, replicas, tensors),
        out_shape=(out, out),
        in_specs=[smem, smem, smem, anywhere, anywhere, anywhere, anywhere],
        out_specs=(vmem, vmem),
        scratch_shapes=scratch,
        compiler_params=pltpu.CompilerParams(collective_id=0, has_side_effects=True),
    )(lengths, live_counts, adapter_index, queries, past_cache, adapter_down, adapter_up)


def solution(mesh):
    in_specs = (
        P(("groups", "replica"), "tensor"),
        P(None, ("groups", "replica"), None, "tensor"),
        P(("groups", "replica")),
        P(("groups", "replica")),
        P(("groups", "replica")),
        P("replica", None, "tensor"),
        P("replica", None, "tensor"),
    )
    out_specs = (P(("groups", "replica"), "tensor"), P(("groups", "replica"), "tensor"))
    body = functools.partial(on_device, mesh.shape["replica"], mesh.shape["tensor"])
    return jax.shard_map(body, mesh=mesh, in_specs=in_specs, out_specs=out_specs, check_vma=False)
```

```python
import functools
import math

import jax
import jax.numpy as jnp
from jax import lax
from jax.experimental import pallas as pl
from jax.experimental.pallas import tpu as pltpu
from jax.sharding import PartitionSpec as P

HEAD_DIM = 128
STAY = 16
SCALING = 2.0
GROUP = 4
REACH = 2
LIMIT = 67043328 - 240 * 1024
MESH = pl.DeviceIdType.MESH
F32 = jnp.float32
BF16 = jnp.bfloat16


def dot_nt(a, b):
    return lax.dot_general(a, b, (((1,), (1,)), ((), ())), preferred_element_type=F32)


def dot_nn(a, b):
    return lax.dot_general(a, b, (((1,), (0,)), ((), ())), preferred_element_type=F32)


def widen(ranks, up):
    high = ranks.astype(BF16)
    low = (ranks - high.astype(F32)).astype(BF16)
    return SCALING * (dot_nn(high, up) + dot_nn(low, up))


def kernel(
    replicas, tensors,
    lengths, live, index, queries, cache, down, up,
    attention, adapted,
    q_in, kv, down_v, up_v, q_rows, o_rows,
    idx_buf, row_out, row_in, row_send, row_back, hot_down, hot_up, rank_m, rank_s,
    local_sem, group_sem,
    idx_s, idx_r, row_s, row_r, back_s, back_r, hd_s, hd_r, hu_s, hu_r, tm_s, tm_r, ts_s, ts_r,
):
    me = lax.axis_index("replica")
    mine = lax.axis_index("tensor")
    slots, cols = queries.shape
    moving = slots - STAY
    context = cache.shape[2]
    key_heads = cache.shape[3] // HEAD_DIM
    heads = cols // HEAD_DIM
    size = heads // key_heads
    count, rank = down.shape[0], down.shape[1]
    groups = STAY // GROUP

    def peer(offset):
        return {"replica": lax.rem(me + offset, replicas)}

    def side(offset):
        return {"tensor": lax.rem(mine + offset, tensors)}

    barrier = pltpu.get_barrier_semaphore()
    for d in range(1, replicas):
        pl.semaphore_signal(barrier, inc=1, device_id=peer(d), device_id_type=MESH)
    for d in range(1, tensors):
        pl.semaphore_signal(barrier, inc=1, device_id=side(d), device_id_type=MESH)

    load_q = pltpu.make_async_copy(queries, q_in, local_sem.at[0])
    load_m = pltpu.make_async_copy(
        cache.at[:, pl.ds(STAY, moving)], kv.at[:, pl.ds(STAY, moving)], local_sem.at[1]
    )
    load_d = pltpu.make_async_copy(down, down_v, local_sem.at[2])
    load_u = pltpu.make_async_copy(up, up_v, local_sem.at[3])
    loads = [
        pltpu.make_async_copy(
            cache.at[:, pl.ds(g * GROUP, GROUP)], kv.at[:, pl.ds(g * GROUP, GROUP)], group_sem.at[g]
        )
        for g in range(groups)
    ]
    load_q.start()
    load_m.start()
    for copy in loads[:2]:
        copy.start()
    load_d.start()
    load_u.start()
    for copy in loads[2:]:
        copy.start()

    def to_peers(source, target, send, recv):
        return [
            pltpu.make_async_remote_copy(
                src_ref=source(d), dst_ref=target.at[d], send_sem=send.at[d - 1],
                recv_sem=recv.at[d - 1], device_id=peer(d), device_id_type=MESH,
            )
            for d in range(1, replicas)
        ]

    def to_sides(buffer, send, recv):
        return [
            pltpu.make_async_remote_copy(
                src_ref=buffer.at[0], dst_ref=buffer.at[d], send_sem=send.at[d - 1],
                recv_sem=recv.at[d - 1], device_id=side(d), device_id_type=MESH,
            )
            for d in range(1, tensors)
        ]

    send_idx = to_peers(lambda d: idx_buf.at[0], idx_buf, idx_s, idx_r)
    send_rows = to_peers(lambda d: row_out.at[d], row_in, row_s, row_r)
    send_hd = to_peers(lambda d: hot_down.at[0], hot_down, hd_s, hd_r)
    send_hu = to_peers(lambda d: hot_up.at[0], hot_up, hu_s, hu_r)

    def straight(d):
        return ((me + d < replicas) & (d <= REACH)) | ((me + d >= replicas) & (replicas - d <= REACH))

    def onward(buffer, send, recv):
        steps = {}
        for d in range(1, replicas):
            options = []
            if d >= REACH and d + 1 < replicas:
                options.append(((me >= d) & (me + 1 < replicas), 1, d + 1, replicas - 1))
            if replicas - d >= REACH and d > 1:
                options.append(((me < d) & (me >= 1), replicas - 1, d - 1, 2 * (replicas - 1)))
            steps[d] = [
                (flag, pltpu.make_async_remote_copy(
                    src_ref=buffer.at[d], dst_ref=buffer.at[slot], send_sem=send.at[base + d - 1],
                    recv_sem=recv.at[slot - 1], device_id=peer(step), device_id_type=MESH,
                ))
                for flag, step, slot, base in options
            ]
        return steps

    pass_hd = onward(hot_down, hd_s, hd_r)
    pass_hu = onward(hot_up, hu_s, hu_r)
    order = sorted(range(1, replicas), key=lambda d: (not pass_hd[d], d))

    def start_if(flag, copy):
        @pl.when(flag)
        def _():
            copy.start()

    def sent_if(flag, copy):
        @pl.when(flag)
        def _():
            copy.wait_send()

    def spread(sends):
        for d in order:
            start_if(straight(d), sends[d - 1])

    def relay(sends, passes):
        for d in order:
            if passes[d]:
                sends[d - 1].wait_recv()
                for flag, copy in passes[d]:
                    start_if(flag, copy)

    def settle(sends, passes):
        for d in order:
            if not passes[d]:
                sends[d - 1].wait_recv()
    send_back = [
        pltpu.make_async_remote_copy(
            src_ref=row_send.at[d], dst_ref=row_back.at[d], send_sem=back_s.at[d - 1],
            recv_sem=back_r.at[d - 1], device_id=peer(replicas - d), device_id_type=MESH,
        )
        for d in range(1, replicas)
    ]
    send_tm = to_sides(rank_m, tm_s, tm_r)
    send_ts = to_sides(rank_s, ts_s, ts_r)

    lane = lax.broadcasted_iota(jnp.int32, (1, 128), 1)
    line = jnp.full((1, 128), -1, jnp.int32)
    for i in range(slots):
        line = jnp.where(lane == i, index[i], line)
    idx_buf[0] = line
    stay_row = lax.broadcasted_iota(jnp.int32, (STAY, 1), 0)
    stay_rel = jnp.zeros((STAY, 1), jnp.int32)
    for i in range(STAY):
        stay_rel = jnp.where(stay_row == i, lax.rem(me - index[i] // count + replicas, replicas), stay_rel)
    move_rel = [lax.rem(index[STAY + j] // count - me + replicas, replicas) for j in range(moving)]

    load_q.wait()
    for h in range(heads):
        q_rows[pl.ds(h, slots, stride=heads), :] = q_in[:, h * HEAD_DIM:(h + 1) * HEAD_DIM].astype(F32)

    head_row = lax.broadcasted_iota(jnp.int32, (heads, 1), 0) // size
    position = lax.broadcasted_iota(jnp.int32, (1, context), 1)

    def attend(requests):
        for n in requests:
            q = q_rows[n * heads:(n + 1) * heads, :]
            wide = jnp.concatenate(
                [jnp.where(head_row == g, q, 0.0) for g in range(key_heads)], axis=1
            ).astype(BF16)
            scores = dot_nt(wide, kv[0, n]) / math.sqrt(HEAD_DIM)
            scores = jnp.where(position < lengths[n], scores, -jnp.inf)
            peak = jnp.max(scores, axis=-1, keepdims=True)
            raised = jnp.exp(scores - peak)
            weights = (raised / jnp.sum(raised, axis=-1, keepdims=True)).astype(BF16)
            mixed = dot_nn(weights, kv[1, n])
            out = jnp.zeros((heads, HEAD_DIM), F32)
            for g in range(key_heads):
                out = jnp.where(head_row == g, mixed[:, g * HEAD_DIM:(g + 1) * HEAD_DIM], out)
            o_rows[n * heads:(n + 1) * heads, :] = out

    def gather_rows(first, number):
        return jnp.concatenate(
            [o_rows[pl.ds(first * heads + h, number, stride=heads), :] for h in range(heads)], axis=1
        )

    load_m.wait()
    attend(range(STAY, slots))
    moved = gather_rows(STAY, moving).astype(BF16)
    attention[STAY:slots, :] = moved
    moved = moved.astype(F32)
    replica_row = lax.broadcasted_iota(jnp.int32, (replicas, 1), 0)
    picked = jnp.zeros((replicas, cols), F32)
    for j in range(moving):
        picked = jnp.where(replica_row == move_rel[j], moved[j:j + 1, :], picked)
    row_in[0] = picked[0:1, :]
    for d in range(1, replicas):
        row_out[d] = picked[d:d + 1, :]

    pl.semaphore_wait(barrier, replicas - 1 + tensors - 1)
    for copy in send_idx:
        copy.start()
    for copy in send_rows:
        copy.start()

    for g in range(groups // 2):
        loads[g].wait()
        attend(range(g * GROUP, (g + 1) * GROUP))

    load_d.wait()
    load_u.wait()
    for copy in send_idx:
        copy.wait_recv()
    table = jnp.concatenate([idx_buf[d] for d in range(replicas)], axis=0)
    here = (table >= 0) & (table // count == me)
    local = jnp.where(here, table - me * count, -1)
    lanes = lax.broadcasted_iota(jnp.int32, table.shape, 1)
    hot = jnp.maximum(jnp.max(jnp.where(lanes < STAY, local, -1)), 0)
    hot_down[0] = down_v[hot]
    hot_up[0] = up_v[hot]
    spread(send_hd)

    asked = jnp.max(jnp.where(lanes >= STAY, local, -1), axis=1, keepdims=True)
    for copy in send_rows:
        copy.wait_recv()
    rows = jnp.concatenate([row_in[d] for d in range(replicas)], axis=0).astype(BF16)
    partial = dot_nt(rows, down_v[...].reshape(count * rank, cols))
    owner = lax.broadcasted_iota(jnp.int32, partial.shape, 1) // rank
    rank_m[0] = jnp.where(owner == asked, partial, 0.0)
    for copy in send_tm:
        copy.start()

    middle = (groups // 2 + groups) // 2
    for g in range(groups // 2, middle):
        loads[g].wait()
        attend(range(g * GROUP, (g + 1) * GROUP))

    relay(send_hd, pass_hd)
    spread(send_hu)

    for copy in send_tm:
        copy.wait_recv()
    total = rank_m[0]
    for d in range(1, tensors):
        total = total + rank_m[d]
    made = widen(total, up_v[...].reshape(count * rank, cols)).astype(BF16).astype(F32)
    row_back[0] = made[0:1, :]
    for d in range(1, replicas):
        row_send[d] = made[d:d + 1, :]
    for copy in send_back:
        copy.start()

    for g in range(middle, groups):
        loads[g].wait()
        attend(range(g * GROUP, (g + 1) * GROUP))
    stay = jnp.where(stay_row < live[0], gather_rows(0, STAY), 0.0).astype(BF16)
    attention[0:STAY, :] = stay

    settle(send_hd, pass_hd)
    partial = dot_nt(stay, hot_down[...].reshape(replicas * rank, cols))
    owner = lax.broadcasted_iota(jnp.int32, partial.shape, 1) // rank
    rank_s[0] = jnp.where(owner == stay_rel, partial, 0.0)
    for copy in send_ts:
        copy.start()

    relay(send_hu, pass_hu)
    for copy in send_back:
        copy.wait_recv()
    back = jnp.concatenate([row_back[d] for d in range(replicas)], axis=0)
    adapted[STAY:slots, :] = jnp.concatenate(
        [
            jnp.sum(jnp.where(replica_row == move_rel[j], back, 0.0), axis=0, keepdims=True)
            for j in range(moving)
        ],
        axis=0,
    ).astype(BF16)

    for copy in send_ts:
        copy.wait_recv()
    total = rank_s[0]
    for d in range(1, tensors):
        total = total + rank_s[d]
    settle(send_hu, pass_hu)
    adapted[0:STAY, :] = widen(total, hot_up[...].reshape(replicas * rank, cols)).astype(BF16)

    for copy in send_idx + send_rows + send_back + send_tm + send_ts:
        copy.wait_send()
    for d in order:
        for copies, passes in ((send_hd, pass_hd), (send_hu, pass_hu)):
            sent_if(straight(d), copies[d - 1])
            for flag, copy in passes[d]:
                sent_if(flag, copy)


def hand_over(attention, adapted, attention_out, adapted_out, sem):
    first = pltpu.make_async_copy(attention, attention_out, sem.at[0])
    second = pltpu.make_async_copy(adapted, adapted_out, sem.at[1])
    first.start()
    second.start()
    first.wait()
    second.wait()


def on_device(replicas, tensors, queries, past_cache, lengths, live_counts, adapter_index, adapter_down, adapter_up):
    slots, cols = queries.shape
    count, rank = adapter_down.shape[0], adapter_down.shape[1]
    heads = cols // HEAD_DIM
    out = jax.ShapeDtypeStruct((slots, cols), BF16)
    held = pltpu.VMEM((slots, cols), BF16)
    smem = pl.BlockSpec(memory_space=pltpu.SMEM)
    anywhere = pl.BlockSpec(memory_space=pl.ANY)
    vmem = pl.BlockSpec(memory_space=pltpu.VMEM)
    dma = pltpu.SemaphoreType.DMA
    rep = dma((max(replicas - 1, 1),))
    ten = dma((max(tensors - 1, 1),))
    three = dma((max(3 * (replicas - 1), 1),))
    scratch = [
        pltpu.VMEM((slots, cols), BF16),
        pltpu.VMEM(past_cache.shape, BF16),
        pltpu.VMEM(adapter_down.shape, BF16),
        pltpu.VMEM(adapter_up.shape, BF16),
        pltpu.VMEM((slots * heads, HEAD_DIM), F32),
        pltpu.VMEM((slots * heads, HEAD_DIM), F32),
        pltpu.VMEM((replicas, 1, 128), jnp.int32),
        pltpu.VMEM((replicas, 1, cols), F32),
        pltpu.VMEM((replicas, 1, cols), F32),
        pltpu.VMEM((replicas, 1, cols), F32),
        pltpu.VMEM((replicas, 1, cols), F32),
        pltpu.VMEM((replicas, rank, cols), BF16),
        pltpu.VMEM((replicas, rank, cols), BF16),
        pltpu.VMEM((tensors, replicas, count * rank), F32),
        pltpu.VMEM((tensors, STAY, replicas * rank), F32),
        dma((4,)),
        dma((STAY // GROUP,)),
        rep, rep, rep, rep, rep, rep, three, rep, three, rep, ten, ten, ten, ten,
    ]
    results = pl.pallas_call(
        functools.partial(kernel, replicas, tensors),
        out_shape=(held, held),
        in_specs=[smem, smem, smem, anywhere, anywhere, anywhere, anywhere],
        out_specs=(vmem, vmem),
        scratch_shapes=scratch,
        compiler_params=pltpu.CompilerParams(collective_id=0, has_side_effects=True, vmem_limit_bytes=LIMIT),
    )(lengths, live_counts, adapter_index, queries, past_cache, adapter_down, adapter_up)
    return pl.pallas_call(
        hand_over,
        out_shape=(out, out),
        in_specs=[vmem, vmem],
        out_specs=(anywhere, anywhere),
        scratch_shapes=[dma((2,))],
        compiler_params=pltpu.CompilerParams(vmem_limit_bytes=4 * 1024 * 1024),
    )(*results)


def solution(mesh):
    in_specs = (
        P(("groups", "replica"), "tensor"),
        P(None, ("groups", "replica"), None, "tensor"),
        P(("groups", "replica")),
        P(("groups", "replica")),
        P(("groups", "replica")),
        P("replica", None, "tensor"),
        P("replica", None, "tensor"),
    )
    out_specs = (P(("groups", "replica"), "tensor"), P(("groups", "replica"), "tensor"))
    body = functools.partial(on_device, mesh.shape["replica"], mesh.shape["tensor"])
    return jax.shard_map(body, mesh=mesh, in_specs=in_specs, out_specs=out_specs, check_vma=False)
```
